32 devices in a mesh: tm: 4 (over y, x), space: 8 (over z, core).
Axes of the slice: x: 2, y: 2, z: 4, core: 2. Of those that a mesh axis runs over, the one named last changes fastest.
Arguments:
- forcing: float32 [4, 64, 16384], P('tm', 'space'), may hold values from -6 to 6
- conductivity: float32 [64, 16384], P('space'), may hold values from 0.1 to 1
Outputs:
- solution: float32 [4, 64, 16384], P('tm', 'space')
The draws below stay inside these ranges and needn't reach their ends.
All inputs are finite; a program needn't handle non-finite values.
Results may differ from the reference program's by a relative error of at most 0.0001.
Values sent between devices are 32-bit elements; how exact they have to be, the bound alone decides.
A program may use at most 64 MiB of HBM per device.

```python
import math
import jax
import jax.numpy as jnp

NY = 16384
ITERS = 3
NT = 4
NX = 64


def block_scale(stream_key, dims, shards, low, high):
    gain = 1.0
    for axis_at, blocks in shards:
        steps = jax.random.uniform(jax.random.fold_in(jax.random.fold_in(stream_key, 6), axis_at), (blocks,), jnp.float32, low / len(shards), high / len(shards))
        gain = gain * jnp.repeat(jnp.exp(steps), dims[axis_at] // blocks).reshape((-1,) + (1,) * (len(dims) - 1 - axis_at))
    return gain


def centred(key, dims, spread, most, split=(), kind=jnp.bfloat16):
    factor_of = block_scale(key, dims, split, -0.22, 0.18) if split else 1.0
    drawn = jax.random.normal(key, dims, jnp.float32) * spread * factor_of
    return jnp.minimum(jnp.maximum(drawn, -most), most).astype(kind)


def setup_inputs(seed: int = 0) -> dict:
    key_list = jax.random.split(jax.random.key(seed), 3)
    return {
        "forcing": centred(key_list[0], (NT, NX, NY), 1.0, 6.0, ((0, 4), (1, 8)), jnp.float32),
        "conductivity": jnp.clip(jnp.exp(math.log(1.0) - 2.3025851 * jax.random.uniform(key_list[1], (NX, NY), jnp.float32) ** block_scale(key_list[1], (NX, NY), ((0, 8),), -0.2, 0.2)), 0.1, 1.0),
    }


def edge_weights(kpad):
    center = kpad[1:-1, 1:-1]
    north = 0.5 * (center + kpad[:-2, 1:-1])
    south = 0.5 * (center + kpad[2:, 1:-1])
    west = 0.5 * (center + kpad[1:-1, :-2])
    east = 0.5 * (center + kpad[1:-1, 2:])
    diag = 1.0 + north + south + west + east
    return (north, south, west, east, diag)

def neighbours(field, north, south, west, east):
    padded = jnp.pad(field, ((0, 0), (1, 1), (1, 1)))
    total = north * padded[:, :-2, 1:-1] + south * padded[:, 2:, 1:-1]
    return total + west * padded[:, 1:-1, :-2] + east * padded[:, 1:-1, 2:]

def operate(field, weights):
    north, south, west, east, diag = weights
    stepped = diag * field - neighbours(field, north, south, west, east)
    earlier = jnp.concatenate([jnp.zeros_like(field[:1]), field[:-1]], 0)
    return jnp.flip(stepped - earlier, 0)

def precondition(field, weights, scale):
    north, south, west, east, diag = weights

    def apply_g(term):
        return scale * neighbours(scale * term, north, south, west, east)
    first = scale * field
    second = apply_g(first)
    third = 2.0 * apply_g(second) - first
    fourth = 2.0 * apply_g(third) - second
    return scale * (first + 0.5 * second + 0.25 * third + 0.125 * fourth)

def reference(forcing, conductivity):
    weights = edge_weights(jnp.pad(conductivity, 1))
    scale = 1.0 / jnp.sqrt(weights[4])
    vec = jnp.flip(forcing, 0)
    vec_old = jnp.zeros_like(vec)
    zvec = precondition(vec, weights, scale)
    gamma = jnp.sqrt(jnp.sum(zvec * vec))
    gamma_old = jnp.float32(1.0)
    wvec = jnp.zeros_like(vec)
    wvec_old = jnp.zeros_like(vec)
    solution = jnp.zeros_like(vec)
    cos_now = jnp.float32(1.0)
    cos_old = jnp.float32(1.0)
    sin_now = jnp.float32(0.0)
    sin_old = jnp.float32(0.0)
    eta = gamma
    for step in range(ITERS):
        zvec = zvec / gamma
        image = operate(zvec, weights)
        delta = jnp.sum(image * zvec)
        vec_new = image - delta / gamma * vec - gamma / gamma_old * vec_old
        zvec_new = precondition(vec_new, weights, scale)
        gamma_new = jnp.sqrt(jnp.sum(zvec_new * vec_new))
        alpha_zero = cos_now * delta - cos_old * sin_now * gamma
        alpha_one = jnp.sqrt(alpha_zero * alpha_zero + gamma_new * gamma_new)
        alpha_two = sin_now * delta + cos_old * cos_now * gamma
        alpha_three = sin_old * gamma
        cos_new = alpha_zero / alpha_one
        sin_new = gamma_new / alpha_one
        wvec_new = (zvec - alpha_three * wvec_old - alpha_two * wvec) / alpha_one
        solution = solution + cos_new * eta * wvec_new
        eta = -sin_new * eta
        vec_old, vec, zvec = (vec, vec_new, zvec_new)
        gamma_old, gamma = (gamma, gamma_new)
        wvec_old, wvec = (wvec, wvec_new)
        cos_old, cos_now, sin_old, sin_now = (cos_now, cos_new, sin_now, sin_new)
    return solution
```

```python
import functools

import jax
import jax.numpy as jnp
from jax import lax
from jax.experimental import pallas as pl
from jax.experimental.pallas import tpu as pltpu
from jax.sharding import PartitionSpec as P

MESH = pl.DeviceIdType.MESH
LANES = 128
SUB = 8


def kernel(
    ntm, nsp, f_hbm, k_hbm, out_hbm,
    fwin, kwin, scl, inv, gn, gs, gw, ge, tau, abuf, bbuf, q0, q1, q2, res, part, red,
    f_send, f_recv, k_send, k_recv, r_send, r_recv, o_send, o_recv, own_sem,
):
    n = ntm * nsp
    mt, ms = lax.axis_index("tm"), lax.axis_index("space")
    me = mt * nsp + ms
    tl, tiles, rows, _ = f_hbm.shape
    steps, width = fwin.shape[0], fwin.shape[1]
    nx = scl.shape[1] - 2 * SUB
    blocks = nx // SUB
    own = tiles // n

    def start_of(d):
        return jnp.minimum(jnp.maximum(d * own - 1, 0), tiles - width)

    def strip(s):
        return pl.ds(pl.multiple_of(SUB + s * rows, SUB), rows)

    def f_copy(d):
        return pltpu.make_async_remote_copy(
            src_ref=f_hbm.at[:, pl.ds(start_of(d), width)],
            dst_ref=fwin.at[pl.ds(mt * tl, tl), :, strip(ms)],
            send_sem=f_send.at[d], recv_sem=f_recv.at[me],
            device_id=(d // nsp, d % nsp), device_id_type=MESH)

    def f_arrival(d):
        return pltpu.make_async_remote_copy(
            src_ref=f_hbm.at[:, pl.ds(0, width)],
            dst_ref=fwin.at[pl.ds((d // nsp) * tl, tl), :, strip(d % nsp)],
            send_sem=f_send.at[d], recv_sem=f_recv.at[d],
            device_id=(d // nsp, d % nsp), device_id_type=MESH)

    def k_copy(s):
        return pltpu.make_async_remote_copy(
            src_ref=k_hbm.at[pl.ds(start_of(mt * nsp + s), width)],
            dst_ref=kwin.at[:, strip(ms)],
            send_sem=k_send.at[s], recv_sem=k_recv.at[ms],
            device_id=(mt, s), device_id_type=MESH)

    def k_arrival(s):
        return pltpu.make_async_remote_copy(
            src_ref=k_hbm.at[pl.ds(0, width)],
            dst_ref=kwin.at[:, strip(s)],
            send_sem=k_send.at[s], recv_sem=k_recv.at[s],
            device_id=(mt, s), device_id_type=MESH)

    def r_copy(d):
        return pltpu.make_async_remote_copy(
            src_ref=part, dst_ref=red.at[me],
            send_sem=r_send.at[d], recv_sem=r_recv.at[me],
            device_id=(d // nsp, d % nsp), device_id_type=MESH)

    def r_arrival(d):
        return pltpu.make_async_remote_copy(
            src_ref=part, dst_ref=red.at[d],
            send_sem=r_send.at[d], recv_sem=r_recv.at[d],
            device_id=(d // nsp, d % nsp), device_id_type=MESH)

    def res_piece(d):
        return res.at[pl.ds((d // nsp) * tl, tl), :,
                      pl.ds(pl.multiple_of((d % nsp) * rows, SUB), rows)]

    def o_copy(d):
        return pltpu.make_async_remote_copy(
            src_ref=res_piece(d), dst_ref=out_hbm.at[:, pl.ds(me * own, own)],
            send_sem=o_send.at[d], recv_sem=o_recv.at[me],
            device_id=(d // nsp, d % nsp), device_id_type=MESH)

    def o_arrival(d):
        return pltpu.make_async_remote_copy(
            src_ref=res_piece(d), dst_ref=out_hbm.at[:, pl.ds(d * own, own)],
            send_sem=o_send.at[d], recv_sem=o_recv.at[d],
            device_id=(d // nsp, d % nsp), device_id_type=MESH)

    def loop(low, high, act):
        def step(j, carry):
            act(j)
            return carry
        lax.fori_loop(low, high, step, 0)

    def peers(act):
        loop(1, n, lambda j: act((me + j) % n))

    def side_peers(act):
        loop(1, nsp, lambda j: act((ms + j) % nsp))

    barrier = pltpu.get_barrier_semaphore()
    peers(lambda d: pl.semaphore_signal(
        barrier, inc=1, device_id=(d // nsp, d % nsp), device_id_type=MESH))
    own_k = pltpu.make_async_copy(
        k_hbm.at[pl.ds(start_of(me), width)], kwin.at[:, strip(ms)], own_sem.at[0])
    own_f = pltpu.make_async_copy(
        f_hbm.at[:, pl.ds(start_of(me), width)],
        fwin.at[pl.ds(mt * tl, tl), :, strip(ms)], own_sem.at[1])
    own_k.start()
    own_f.start()
    zero = jnp.zeros((SUB, LANES), jnp.float32)
    for edge in (0, SUB + nx):
        for c in range(width):
            for ref in (kwin, scl):
                ref[c, edge:edge + SUB, :] = zero
            for ref in (tau, abuf, bbuf, q0, q1, q2):
                for s in range(steps):
                    ref[s, c, edge:edge + SUB, :] = zero
    pl.semaphore_wait(barrier, n - 1)

    side_peers(lambda s: k_copy(s).start())
    peers(lambda d: f_copy(d).start())
    own_k.wait()
    side_peers(lambda s: k_arrival(s).wait_recv())

    lane = lax.broadcasted_iota(jnp.int32, (SUB, LANES), 1)
    first, last = lane == 0, lane == LANES - 1

    def lefts(xs):
        turned = [pltpu.roll(x, 1, 1) for x in xs]
        return [jnp.where(first, turned[c - 1] if c else 0.0, turned[c]) for c in range(width)]

    def rights(xs):
        turned = [pltpu.roll(x, LANES - 1, 1) for x in xs] + [0.0]
        return [jnp.where(last, turned[c + 1], turned[c]) for c in range(width)]

    def near(i, offset):
        return pl.ds(SUB + SUB * i + offset, SUB)

    def at(i):
        return pl.ds(pl.multiple_of(SUB + SUB * i, SUB), SUB)

    def flat(i):
        return pl.ds(pl.multiple_of(SUB * i, SUB), SUB)

    def weights_first(i):
        ks = [kwin[c, at(i), :] for c in range(width)]
        for c, (k, l, r) in enumerate(zip(ks, lefts(ks), rights(ks))):
            up, down = kwin[c, near(i, -1), :], kwin[c, near(i, 1), :]
            diag = 1.0 + 0.5 * (k + up) + 0.5 * (k + down) + 0.5 * (k + l) + 0.5 * (k + r)
            scl[c, at(i), :] = 1.0 / jnp.sqrt(diag)
            inv[c, flat(i), :] = 1.0 / diag

    def weights_second(i):
        ks = [kwin[c, at(i), :] for c in range(width)]
        ss = [scl[c, at(i), :] for c in range(width)]
        quads = zip(ks, lefts(ks), rights(ks), ss, lefts(ss), rights(ss))
        for c, (k, kl, kr, s, sl, sr) in enumerate(quads):
            half = 0.5 * s
            gn[c, flat(i), :] = half * (k + kwin[c, near(i, -1), :]) * scl[c, near(i, -1), :]
            gs[c, flat(i), :] = half * (k + kwin[c, near(i, 1), :]) * scl[c, near(i, 1), :]
            gw[c, flat(i), :] = half * (k + kl) * sl
            ge[c, flat(i), :] = half * (k + kr) * sr

    loop(0, blocks, weights_first)
    loop(0, blocks, weights_second)

    own_f.wait()
    peers(lambda d: f_arrival(d).wait_recv())

    def scale_in(i):
        for c in range(width):
            s = scl[c, at(i), :]
            for t in range(steps):
                tau[t, c, at(i), :] = s * fwin[steps - 1 - t, c, at(i), :]

    loop(0, blocks, scale_in)

    offset = me * own - start_of(me)
    mine = [jnp.where(jnp.logical_and(c >= offset, c < offset + own), 1.0, 0.0)
            for c in range(width)]

    def sweep(src, use):
        def block(i, total):
            xs = [[src[t, c, at(i), :] for c in range(width)] for t in range(steps)]
            ls = [lefts(x) for x in xs]
            rs = [rights(x) for x in xs]
            for c in range(width):
                wn, wso = gn[c, flat(i), :], gs[c, flat(i), :]
                ww, we = gw[c, flat(i), :], ge[c, flat(i), :]
                out = [
                    wn * src[t, c, near(i, -1), :] + wso * src[t, c, near(i, 1), :]
                    + (ww * ls[t][c] + we * rs[t][c])
                    for t in range(steps)
                ]
                term = use(c, i, [xs[t][c] for t in range(steps)], out)
                if term is not None:
                    total = total + mine[c] * term
            return total
        return lax.fori_loop(0, blocks, block, zero)

    def precondition(q):
        def one(c, i, x, g):
            for t in range(steps):
                abuf[t, c, at(i), :] = 0.5 * (x[t] + g[t])

        def two(c, i, x, g):
            for t in range(steps):
                bbuf[t, c, at(i), :] = 0.125 * tau[t, c, at(i), :] + g[t]

        def three(c, i, x, g):
            term = zero
            for t in range(steps):
                v = tau[t, c, at(i), :]
                y = 0.75 * v + g[t]
                q[t, c, at(i), :] = y
                term = term + v * y
            return term

        sweep(tau, one)
        sweep(abuf, two)
        return sweep(bbuf, three)

    def operate(q):
        def use(c, i, x, g):
            shrink = inv[c, flat(i), :]
            term = zero
            for t in range(steps):
                y = x[t] - g[t]
                if t:
                    y = y - shrink * x[t - 1]
                tau[steps - 1 - t, c, at(i), :] = y
                term = term + y * x[steps - 1 - t]
            return term
        return sweep(q, use)

    precondition(q0)
    m1 = operate(q0)
    m2 = precondition(q1)
    m3 = operate(q1)
    m4 = precondition(q2)
    m5 = operate(q2)

    def norm_one(c, i, x, g):
        term = zero
        for t in range(steps):
            abuf[t, c, at(i), :] = g[t]
            term = term + (x[t] * (0.75 * x[t] + 0.125 * g[t]) + 0.5 * (g[t] * g[t]))
        return term

    def norm_two(c, i, x, g):
        term = zero
        for t in range(steps):
            term = term + 0.5 * (x[t] * g[t])
        return term

    m6 = sweep(tau, norm_one) + sweep(abuf, norm_two)

    row = jnp.zeros((1, LANES), jnp.float32)
    lane1 = lax.broadcasted_iota(jnp.int32, (1, LANES), 1)
    for j, m in enumerate((m1, m2, m3, m4, m5, m6)):
        value = jnp.sum(jnp.sum(m, axis=0, keepdims=True), axis=1, keepdims=True)
        row = jnp.where(lane1 == j, value, row)
    part[...] = row
    red[me] = row
    peers(lambda d: r_copy(d).start())
    peers(lambda d: r_arrival(d).wait_recv())
    total = lax.fori_loop(0, n, lambda j, acc: acc + red[j], jnp.zeros((1, LANES), jnp.float32))
    n1, n2, n3, n4, n5, n6 = [
        jnp.sum(jnp.where(lane1 == j, total, 0.0), axis=1, keepdims=True) for j in range(6)]

    tiny = 1e-7
    d1 = jnp.maximum(n2, 1e-37)
    l21, l31 = n3 / d1, n4 / d1
    d2 = jnp.maximum(n4 - l21 * n3, jnp.maximum(tiny * n4, 1e-37))
    e32 = n5 - l31 * n3
    l32 = e32 / d2
    d3 = jnp.maximum(n6 - l31 * n4 - l32 * e32, jnp.maximum(tiny * n6, 1e-37))
    y2 = n2 - l21 * n1
    y3 = n3 - l31 * n1 - l32 * y2
    a2 = y3 / d3
    a1 = y2 / d2 - l32 * a2
    a0 = n1 / d1 - l21 * a1 - l31 * a2

    def finish(i):
        for c in range(own):
            s = scl[offset + c, at(i), :]
            s0, s1, s2 = a0 * s, a1 * s, a2 * s
            for t in range(steps):
                res[t, c, flat(i), :] = (
                    s0 * q0[t, offset + c, at(i), :] + s1 * q1[t, offset + c, at(i), :]
                    + s2 * q2[t, offset + c, at(i), :])

    loop(0, blocks, finish)
    own_out = pltpu.make_async_copy(
        res_piece(me), out_hbm.at[:, pl.ds(me * own, own)], own_sem.at[2])
    own_out.start()
    peers(lambda d: o_copy(d).start())
    side_peers(lambda s: k_copy(s).wait_send())
    peers(lambda d: f_copy(d).wait_send())
    peers(lambda d: r_copy(d).wait_send())
    own_out.wait()
    peers(lambda d: o_arrival(d).wait_recv())
    peers(lambda d: o_copy(d).wait_send())


def solution(mesh):
    ntm, nsp = mesh.shape["tm"], mesh.shape["space"]
    n = ntm * nsp

    def body(forcing, conductivity):
        tl, rows, columns = forcing.shape
        tiles = columns // LANES
        own = tiles // n
        width = min(own + 2, tiles)
        steps, nx = tl * ntm, rows * nsp
        f = forcing.reshape(tl, rows, tiles, LANES).transpose(0, 2, 1, 3)
        k = conductivity.reshape(rows, tiles, LANES).transpose(1, 0, 2)
        padded = pltpu.VMEM((width, nx + 2 * SUB, LANES), jnp.float32)
        plain = pltpu.VMEM((width, nx, LANES), jnp.float32)
        field = pltpu.VMEM((steps, width, nx + 2 * SUB, LANES), jnp.float32)
        dma = pltpu.SemaphoreType.DMA
        out = pl.pallas_call(
            functools.partial(kernel, ntm, nsp),
            out_shape=jax.ShapeDtypeStruct((tl, tiles, rows, LANES), jnp.float32),
            in_specs=[pl.BlockSpec(memory_space=pltpu.HBM)] * 2,
            out_specs=pl.BlockSpec(memory_space=pltpu.HBM),
            scratch_shapes=[
                field, padded, padded, plain, plain, plain, plain, plain,
                field, field, field, field, field, field,
                pltpu.VMEM((steps, own, nx, LANES), jnp.float32),
                pltpu.VMEM((1, LANES), jnp.float32),
                pltpu.VMEM((n, 1, LANES), jnp.float32),
                dma((n,)), dma((n,)), dma((nsp,)), dma((nsp,)),
                dma((n,)), dma((n,)), dma((n,)), dma((n,)), dma((3,)),
            ],
            compiler_params=pltpu.CompilerParams(collective_id=0, has_side_effects=True),
        )(f, k)
        return out.transpose(0, 2, 1, 3).reshape(tl, rows, columns)

    return jax.shard_map(
        body,
        mesh=mesh,
        in_specs=(P("tm", "space", None), P("space", None)),
        out_specs=P("tm", "space", None),
        check_vma=False,
    )
```

```python
import functools

import jax
import jax.numpy as jnp
from jax import lax
from jax.experimental import pallas as pl
from jax.experimental.pallas import tpu as pltpu
from jax.sharding import PartitionSpec as P

MESH = pl.DeviceIdType.MESH
LANES = 128
SUB = 8


def kernel(
    ntm, nsp, f_hbm, k_hbm, out_hbm,
    fstage, kloc, kstage, fwin, kwin, scl, inv, gn, gs, gw, ge, tau, abuf, bbuf, q0, q1, q2, res, part, red,
    f_send, f_recv, k_send, k_recv, r_send, r_recv, o_send, o_recv, own_sem,
):
    n = ntm * nsp
    mt, ms = lax.axis_index("tm"), lax.axis_index("space")
    me = mt * nsp + ms
    tl, _, own, rows, _ = f_hbm.shape
    steps, width = fwin.shape[0], fwin.shape[1]
    nx = scl.shape[1] - 2 * SUB
    blocks = nx // SUB

    def strip(s):
        return pl.ds(pl.multiple_of(SUB + s * rows, SUB), rows)

    def f_copy(d):
        return pltpu.make_async_remote_copy(
            src_ref=fstage.at[:, d],
            dst_ref=fwin.at[pl.ds(mt * tl, tl), :, strip(ms)],
            send_sem=f_send.at[d], recv_sem=f_recv.at[me],
            device_id=(d // nsp, d % nsp), device_id_type=MESH)

    def f_arrival(d):
        return pltpu.make_async_remote_copy(
            src_ref=fstage.at[:, d],
            dst_ref=fwin.at[pl.ds((d // nsp) * tl, tl), :, strip(d % nsp)],
            send_sem=f_send.at[d], recv_sem=f_recv.at[d],
            device_id=(d // nsp, d % nsp), device_id_type=MESH)

    def k_copy(s):
        return pltpu.make_async_remote_copy(
            src_ref=kstage.at[s],
            dst_ref=kwin.at[:, strip(ms)],
            send_sem=k_send.at[s], recv_sem=k_recv.at[ms],
            device_id=(mt, s), device_id_type=MESH)

    def k_arrival(s):
        return pltpu.make_async_remote_copy(
            src_ref=kstage.at[s],
            dst_ref=kwin.at[:, strip(s)],
            send_sem=k_send.at[s], recv_sem=k_recv.at[s],
            device_id=(mt, s), device_id_type=MESH)

    def r_copy(d):
        return pltpu.make_async_remote_copy(
            src_ref=part, dst_ref=red.at[me],
            send_sem=r_send.at[d], recv_sem=r_recv.at[me],
            device_id=(d // nsp, d % nsp), device_id_type=MESH)

    def r_arrival(d):
        return pltpu.make_async_remote_copy(
            src_ref=part, dst_ref=red.at[d],
            send_sem=r_send.at[d], recv_sem=r_recv.at[d],
            device_id=(d // nsp, d % nsp), device_id_type=MESH)

    def res_piece(d):
        return res.at[pl.ds((d // nsp) * tl, tl), :,
                      pl.ds(pl.multiple_of((d % nsp) * rows, SUB), rows)]

    def o_copy(d):
        return pltpu.make_async_remote_copy(
            src_ref=res_piece(d), dst_ref=out_hbm.at[:, pl.ds(me * own, own)],
            send_sem=o_send.at[d], recv_sem=o_recv.at[me],
            device_id=(d // nsp, d % nsp), device_id_type=MESH)

    def o_arrival(d):
        return pltpu.make_async_remote_copy(
            src_ref=res_piece(d), dst_ref=out_hbm.at[:, pl.ds(d * own, own)],
            send_sem=o_send.at[d], recv_sem=o_recv.at[d],
            device_id=(d // nsp, d % nsp), device_id_type=MESH)

    def loop(low, high, act):
        def step(j, carry):
            act(j)
            return carry
        lax.fori_loop(low, high, step, 0)

    def peers(act):
        loop(1, n, lambda j: act((me + j) % n))

    def side_peers(act):
        loop(1, nsp, lambda j: act((ms + j) % nsp))

    barrier = pltpu.get_barrier_semaphore()
    peers(lambda d: pl.semaphore_signal(
        barrier, inc=1, device_id=(d // nsp, d % nsp), device_id_type=MESH))
    loads = [
        pltpu.make_async_copy(f_hbm, fstage.at[:, :, pl.ds(0, own)], own_sem.at[0]),
        pltpu.make_async_copy(k_hbm, kloc, own_sem.at[1]),
        pltpu.make_async_copy(
            k_hbm.at[pl.ds(mt * nsp, nsp)], kstage.at[:, pl.ds(0, own)], own_sem.at[2]),
    ]
    for load in loads:
        load.start()
    zero = jnp.zeros((SUB, LANES), jnp.float32)
    for edge in (0, SUB + nx):
        for c in range(width):
            for ref in (kwin, scl):
                ref[c, edge:edge + SUB, :] = zero
            for ref in (tau, abuf, bbuf, q0, q1, q2):
                for s in range(steps):
                    ref[s, c, edge:edge + SUB, :] = zero
    lane = lax.broadcasted_iota(jnp.int32, (SUB, LANES), 1)
    first, last, ahead = lane == 0, lane == LANES - 1, lane < LANES // 2

    def beside(d, right, left):
        return jnp.where(ahead, right * jnp.where(d < n - 1, 1.0, 0.0),
                         left * jnp.where(d > 0, 1.0, 0.0))

    def after(d):
        return jnp.minimum(d + 1, n - 1)

    def before(d):
        return jnp.maximum(d - 1, 0)

    for load in loads:
        load.wait()

    def overlap_k(s):
        d = mt * nsp + s
        for r in range(0, rows, SUB):
            kstage[s, own, r:r + SUB, :] = beside(
                d, kloc[after(d), 0, r:r + SUB, :], kloc[before(d), own - 1, r:r + SUB, :])

    def overlap_f(d):
        for t in range(tl):
            for r in range(0, rows, SUB):
                fstage[t, d, own, r:r + SUB, :] = beside(
                    d, fstage[t, after(d), 0, r:r + SUB, :],
                    fstage[t, before(d), own - 1, r:r + SUB, :])

    loop(0, nsp, overlap_k)
    loop(0, n, overlap_f)
    own_k = pltpu.make_async_copy(kstage.at[ms], kwin.at[:, strip(ms)], own_sem.at[0])
    own_f = pltpu.make_async_copy(
        fstage.at[:, me], fwin.at[pl.ds(mt * tl, tl), :, strip(ms)], own_sem.at[1])
    pl.semaphore_wait(barrier, n - 1)

    side_peers(lambda s: k_copy(s).start())
    peers(lambda d: f_copy(d).start())
    own_k.start()
    own_f.start()
    own_k.wait()
    side_peers(lambda s: k_arrival(s).wait_recv())

    def lefts(xs):
        turned = [pltpu.roll(x, 1, 1) for x in xs]
        return [jnp.where(first, turned[c - 1], turned[c]) for c in range(width)]

    def rights(xs):
        turned = [pltpu.roll(x, LANES - 1, 1) for x in xs]
        return [jnp.where(last, turned[(c + 1) % width], turned[c]) for c in range(width)]

    def near(i, offset):
        return pl.ds(SUB + SUB * i + offset, SUB)

    def at(i):
        return pl.ds(pl.multiple_of(SUB + SUB * i, SUB), SUB)

    def flat(i):
        return pl.ds(pl.multiple_of(SUB * i, SUB), SUB)

    inside = beside(me, jnp.ones((SUB, LANES), jnp.float32), jnp.ones((SUB, LANES), jnp.float32))

    def weights_first(i):
        ks = [kwin[c, at(i), :] for c in range(width)]
        for c, (k, l, r) in enumerate(zip(ks, lefts(ks), rights(ks))):
            up, down = kwin[c, near(i, -1), :], kwin[c, near(i, 1), :]
            diag = 1.0 + 0.5 * (k + up) + 0.5 * (k + down) + 0.5 * (k + l) + 0.5 * (k + r)
            scale = 1.0 / jnp.sqrt(diag)
            scl[c, at(i), :] = scale * inside if c == own else scale
            inv[c, flat(i), :] = 1.0 / diag

    def weights_second(i):
        ks = [kwin[c, at(i), :] for c in range(width)]
        ss = [scl[c, at(i), :] for c in range(width)]
        quads = zip(ks, lefts(ks), rights(ks), ss, lefts(ss), rights(ss))
        for c, (k, kl, kr, s, sl, sr) in enumerate(quads):
            half = 0.5 * s
            gn[c, flat(i), :] = half * (k + kwin[c, near(i, -1), :]) * scl[c, near(i, -1), :]
            gs[c, flat(i), :] = half * (k + kwin[c, near(i, 1), :]) * scl[c, near(i, 1), :]
            gw[c, flat(i), :] = half * (k + kl) * sl
            ge[c, flat(i), :] = half * (k + kr) * sr

    loop(0, blocks, weights_first)
    loop(0, blocks, weights_second)

    own_f.wait()
    peers(lambda d: f_arrival(d).wait_recv())

    def scale_in(i):
        for c in range(width):
            s = scl[c, at(i), :]
            for t in range(steps):
                tau[t, c, at(i), :] = s * fwin[steps - 1 - t, c, at(i), :]

    loop(0, blocks, scale_in)

    def sweep(src, use):
        def block(i, total):
            xs, down, up = {}, {}, {}

            def fetch(c, t):
                if (c, t) not in xs:
                    x = src[t, c, at(i), :]
                    xs[c, t], down[c, t], up[c, t] = (
                        x, pltpu.roll(x, 1, 1), pltpu.roll(x, LANES - 1, 1))

            for c in range(width):
                wn, wso = gn[c, flat(i), :], gs[c, flat(i), :]
                ww, we = gw[c, flat(i), :], ge[c, flat(i), :]
                out = []
                for t in range(steps):
                    for b in (c - 1) % width, c, (c + 1) % width:
                        fetch(b, t)
                    left = jnp.where(first, down[(c - 1) % width, t], down[c, t])
                    right = jnp.where(last, up[(c + 1) % width, t], up[c, t])
                    out.append(
                        wn * src[t, c, near(i, -1), :] + wso * src[t, c, near(i, 1), :]
                        + (ww * left + we * right))
                term = use(c, i, [xs[c, t] for t in range(steps)], out)
                if term is not None and c < own:
                    total = total + term
            return total
        return lax.fori_loop(0, blocks, block, zero)

    def precondition(q):
        def one(c, i, x, g):
            for t in range(steps):
                abuf[t, c, at(i), :] = 0.5 * (x[t] + g[t])

        def two(c, i, x, g):
            for t in range(steps):
                bbuf[t, c, at(i), :] = 0.125 * tau[t, c, at(i), :] + g[t]

        def three(c, i, x, g):
            term = zero
            for t in range(steps):
                v = tau[t, c, at(i), :]
                y = 0.75 * v + g[t]
                q[t, c, at(i), :] = y
                term = term + v * y
            return term

        sweep(tau, one)
        sweep(abuf, two)
        return sweep(bbuf, three)

    def operate(q):
        def use(c, i, x, g):
            shrink = inv[c, flat(i), :]
            term = zero
            for t in range(steps):
                y = x[t] - g[t]
                if t:
                    y = y - shrink * x[t - 1]
                tau[steps - 1 - t, c, at(i), :] = y
                term = term + y * x[steps - 1 - t]
            return term
        return sweep(q, use)

    precondition(q0)
    m1 = operate(q0)
    m2 = precondition(q1)
    m3 = operate(q1)
    m4 = precondition(q2)
    m5 = operate(q2)

    def norm_one(c, i, x, g):
        term = zero
        for t in range(steps):
            abuf[t, c, at(i), :] = g[t]
            term = term + (x[t] * (0.75 * x[t] + 0.125 * g[t]) + 0.5 * (g[t] * g[t]))
        return term

    def norm_two(c, i, x, g):
        term = zero
        for t in range(steps):
            term = term + 0.5 * (x[t] * g[t])
        return term

    m6 = sweep(tau, norm_one) + sweep(abuf, norm_two)

    row = jnp.zeros((1, LANES), jnp.float32)
    lane1 = lax.broadcasted_iota(jnp.int32, (1, LANES), 1)
    for j, m in enumerate((m1, m2, m3, m4, m5, m6)):
        value = jnp.sum(jnp.sum(m, axis=0, keepdims=True), axis=1, keepdims=True)
        row = jnp.where(lane1 == j, value, row)
    part[...] = row
    red[me] = row
    peers(lambda d: r_copy(d).start())
    peers(lambda d: r_arrival(d).wait_recv())
    total = lax.fori_loop(0, n, lambda j, acc: acc + red[j], jnp.zeros((1, LANES), jnp.float32))
    n1, n2, n3, n4, n5, n6 = [
        jnp.sum(jnp.where(lane1 == j, total, 0.0), axis=1, keepdims=True) for j in range(6)]

    tiny = 1e-7
    d1 = jnp.maximum(n2, 1e-37)
    l21, l31 = n3 / d1, n4 / d1
    d2 = jnp.maximum(n4 - l21 * n3, jnp.maximum(tiny * n4, 1e-37))
    e32 = n5 - l31 * n3
    l32 = e32 / d2
    d3 = jnp.maximum(n6 - l31 * n4 - l32 * e32, jnp.maximum(tiny * n6, 1e-37))
    y2 = n2 - l21 * n1
    y3 = n3 - l31 * n1 - l32 * y2
    a2 = y3 / d3
    a1 = y2 / d2 - l32 * a2
    a0 = n1 / d1 - l21 * a1 - l31 * a2

    def finish(i):
        for c in range(own):
            s = scl[c, at(i), :]
            s0, s1, s2 = a0 * s, a1 * s, a2 * s
            for t in range(steps):
                res[t, c, flat(i), :] = (
                    s0 * q0[t, c, at(i), :] + s1 * q1[t, c, at(i), :]
                    + s2 * q2[t, c, at(i), :])

    loop(0, blocks, finish)
    own_out = pltpu.make_async_copy(
        res_piece(me), out_hbm.at[:, pl.ds(me * own, own)], own_sem.at[2])
    own_out.start()
    peers(lambda d: o_copy(d).start())
    side_peers(lambda s: k_copy(s).wait_send())
    peers(lambda d: f_copy(d).wait_send())
    peers(lambda d: r_copy(d).wait_send())
    own_out.wait()
    peers(lambda d: o_arrival(d).wait_recv())
    peers(lambda d: o_copy(d).wait_send())


def solution(mesh):
    ntm, nsp = mesh.shape["tm"], mesh.shape["space"]
    n = ntm * nsp

    def body(forcing, conductivity):
        tl, rows, columns = forcing.shape
        tiles = columns // LANES
        own = tiles // n
        width = own + 1
        steps, nx = tl * ntm, rows * nsp
        f = forcing.reshape(tl, rows, n, own, LANES).transpose(0, 2, 3, 1, 4)
        k = conductivity.reshape(rows, n, own, LANES).transpose(1, 2, 0, 3)
        padded = pltpu.VMEM((width, nx + 2 * SUB, LANES), jnp.float32)
        plain = pltpu.VMEM((width, nx, LANES), jnp.float32)
        field = pltpu.VMEM((steps, width, nx + 2 * SUB, LANES), jnp.float32)
        dma = pltpu.SemaphoreType.DMA
        out = pl.pallas_call(
            functools.partial(kernel, ntm, nsp),
            out_shape=jax.ShapeDtypeStruct((tl, tiles, rows, LANES), jnp.float32),
            in_specs=[pl.BlockSpec(memory_space=pltpu.HBM)] * 2,
            out_specs=pl.BlockSpec(memory_space=pl.ANY),
            scratch_shapes=[
                pltpu.VMEM((tl, n, width, rows, LANES), jnp.float32),
                pltpu.VMEM((n, own, rows, LANES), jnp.float32),
                pltpu.VMEM((nsp, width, rows, LANES), jnp.float32),
                field, padded, padded, plain, plain, plain, plain, plain,
                field, field, field, field, field, field,
                pltpu.VMEM((steps, own, nx, LANES), jnp.float32),
                pltpu.VMEM((1, LANES), jnp.float32),
                pltpu.VMEM((n, 1, LANES), jnp.float32),
                dma((n,)), dma((n,)), dma((nsp,)), dma((nsp,)),
                dma((n,)), dma((n,)), dma((n,)), dma((n,)), dma((3,)),
            ],
            compiler_params=pltpu.CompilerParams(
                collective_id=0, has_side_effects=True, vmem_limit_bytes=24 * 1024 * 1024),
        )(f, k)
        return out.transpose(0, 2, 1, 3).reshape(tl, rows, columns)

    return jax.shard_map(
        body,
        mesh=mesh,
        in_specs=(P("tm", "space", None), P("space", None)),
        out_specs=P("tm", "space", None),
        check_vma=False,
    )
```

```python
import functools

import jax
import jax.numpy as jnp
from jax import lax
from jax.experimental import pallas as pl
from jax.experimental.pallas import tpu as pltpu
from jax.sharding import PartitionSpec as P

MESH = pl.DeviceIdType.MESH
LANES = 128
SUB = 8


def kernel(
    ntm, nsp, f_hbm, k_hbm, out_hbm,
    fstage, kloc, kstage, fwin, kwin, scl, inv, gn, gs, gw, ge, tau, abuf, bbuf, q0, q1, q2, res, part, red,
    f_sem, k_sem, r_sem, o_sem, own_sem,
):
    n = ntm * nsp
    mt, ms = lax.axis_index("tm"), lax.axis_index("space")
    me = mt * nsp + ms
    tl, _, own, rows, _ = f_hbm.shape
    steps, width = fwin.shape[0], fwin.shape[1]
    nx = scl.shape[1] - 2 * SUB
    blocks = nx // SUB

    def strip(s):
        return pl.ds(pl.multiple_of(SUB + s * rows, SUB), rows)

    def send(src, dst, sems, dt, ds):
        return pltpu.make_async_remote_copy(
            src_ref=src, dst_ref=dst, send_sem=sems.at[0], recv_sem=sems.at[1],
            device_id=(dt, ds), device_id_type=MESH)

    def f_copy(dt, ds):
        return send(fstage.at[:, dt * nsp + ds],
                    fwin.at[pl.ds(mt * tl, tl), :, strip(ms)], f_sem, dt, ds)

    def k_copy(dt, ds):
        return send(kstage.at[ds], kwin.at[:, strip(ms)], k_sem, dt, ds)

    def r_copy(dt, ds):
        return send(part, red.at[me], r_sem, dt, ds)

    def res_piece(dt, ds):
        return res.at[pl.ds(dt * tl, tl), :, pl.ds(pl.multiple_of(ds * rows, SUB), rows)]

    def o_copy(dt, ds):
        return send(res_piece(dt, ds), out_hbm.at[:, pl.ds(me * own, own)], o_sem, dt, ds)

    def await_bytes(ref, sem):
        pltpu.make_async_copy(ref, ref, sem).wait()

    def loop(low, high, act):
        def step(j, carry):
            act(j)
            return carry
        lax.fori_loop(low, high, step, 0)

    def turn(at, by, size):
        moved = at + by
        return jnp.where(moved >= size, moved - size, moved)

    def peers(act):
        for js in range(nsp):
            ds = turn(ms, js, nsp)
            for jt in range(ntm):
                if js or jt:
                    act(turn(mt, jt, ntm), ds)

    def side_peers(act):
        for js in range(1, nsp):
            act(mt, turn(ms, js, nsp))

    barrier = pltpu.get_barrier_semaphore()
    peers(lambda dt, ds: pl.semaphore_signal(
        barrier, inc=1, device_id=(dt, ds), device_id_type=MESH))
    loads = [
        pltpu.make_async_copy(f_hbm, fstage.at[:, :, pl.ds(0, own)], own_sem.at[0]),
        pltpu.make_async_copy(k_hbm, kloc, own_sem.at[1]),
        pltpu.make_async_copy(
            k_hbm.at[pl.ds(mt * nsp, nsp)], kstage.at[:, pl.ds(0, own)], own_sem.at[2]),
    ]
    for load in loads:
        load.start()
    zero = jnp.zeros((SUB, LANES), jnp.float32)
    for edge in (0, SUB + nx):
        for c in range(width):
            for ref in (kwin, scl):
                ref[c, edge:edge + SUB, :] = zero
            for ref in (tau, abuf, bbuf, q0, q1, q2):
                for s in range(steps):
                    ref[s, c, edge:edge + SUB, :] = zero
    lane = lax.broadcasted_iota(jnp.int32, (SUB, LANES), 1)
    first, last, ahead = lane == 0, lane == LANES - 1, lane < LANES // 2

    def beside(d, right, left):
        return jnp.where(ahead, right * jnp.where(d < n - 1, 1.0, 0.0),
                         left * jnp.where(d > 0, 1.0, 0.0))

    def after(d):
        return jnp.minimum(d + 1, n - 1)

    def before(d):
        return jnp.maximum(d - 1, 0)

    for load in loads:
        load.wait()

    def overlap_k(s):
        d = mt * nsp + s
        for r in range(0, rows, SUB):
            kstage[s, own, r:r + SUB, :] = beside(
                d, kloc[after(d), 0, r:r + SUB, :], kloc[before(d), own - 1, r:r + SUB, :])

    def overlap_f(d):
        for t in range(tl):
            for r in range(0, rows, SUB):
                fstage[t, d, own, r:r + SUB, :] = beside(
                    d, fstage[t, after(d), 0, r:r + SUB, :],
                    fstage[t, before(d), own - 1, r:r + SUB, :])

    loop(0, nsp, overlap_k)
    loop(0, n, overlap_f)
    own_k = pltpu.make_async_copy(kstage.at[ms], kwin.at[:, strip(ms)], k_sem.at[1])
    own_f = pltpu.make_async_copy(
        fstage.at[:, me], fwin.at[pl.ds(mt * tl, tl), :, strip(ms)], f_sem.at[1])
    pl.semaphore_wait(barrier, n - 1)

    side_peers(lambda dt, ds: k_copy(dt, ds).start())
    peers(lambda dt, ds: f_copy(dt, ds).start())
    own_k.start()
    own_f.start()
    await_bytes(kwin.at[:, pl.ds(SUB, nx)], k_sem.at[1])

    def lefts(xs):
        turned = [pltpu.roll(x, 1, 1) for x in xs]
        return [jnp.where(first, turned[c - 1], turned[c]) for c in range(width)]

    def rights(xs):
        turned = [pltpu.roll(x, LANES - 1, 1) for x in xs]
        return [jnp.where(last, turned[(c + 1) % width], turned[c]) for c in range(width)]

    def near(i, offset):
        return pl.ds(SUB + SUB * i + offset, SUB)

    def at(i):
        return pl.ds(pl.multiple_of(SUB + SUB * i, SUB), SUB)

    def flat(i):
        return pl.ds(pl.multiple_of(SUB * i, SUB), SUB)

    inside = beside(me, jnp.ones((SUB, LANES), jnp.float32), jnp.ones((SUB, LANES), jnp.float32))

    def weights_first(i):
        ks = [kwin[c, at(i), :] for c in range(width)]
        for c, (k, l, r) in enumerate(zip(ks, lefts(ks), rights(ks))):
            up, down = kwin[c, near(i, -1), :], kwin[c, near(i, 1), :]
            diag = 1.0 + 0.5 * (k + up) + 0.5 * (k + down) + 0.5 * (k + l) + 0.5 * (k + r)
            scale = 1.0 / jnp.sqrt(diag)
            scl[c, at(i), :] = scale * inside if c == own else scale
            inv[c, flat(i), :] = 1.0 / diag

    def weights_second(i):
        ks = [kwin[c, at(i), :] for c in range(width)]
        ss = [scl[c, at(i), :] for c in range(width)]
        quads = zip(ks, lefts(ks), rights(ks), ss, lefts(ss), rights(ss))
        for c, (k, kl, kr, s, sl, sr) in enumerate(quads):
            half = 0.5 * s
            gn[c, flat(i), :] = half * (k + kwin[c, near(i, -1), :]) * scl[c, near(i, -1), :]
            gs[c, flat(i), :] = half * (k + kwin[c, near(i, 1), :]) * scl[c, near(i, 1), :]
            gw[c, flat(i), :] = half * (k + kl) * sl
            ge[c, flat(i), :] = half * (k + kr) * sr

    loop(0, blocks, weights_first)
    loop(0, blocks, weights_second)

    await_bytes(fwin.at[:, :, pl.ds(SUB, nx)], f_sem.at[1])

    def scale_in(i):
        for c in range(width):
            s = scl[c, at(i), :]
            for t in range(steps):
                tau[t, c, at(i), :] = s * fwin[steps - 1 - t, c, at(i), :]

    loop(0, blocks, scale_in)

    def sweep(src, use):
        def block(i, total):
            xs, down, up = {}, {}, {}

            def fetch(c, t):
                if (c, t) not in xs:
                    x = src[t, c, at(i), :]
                    xs[c, t], down[c, t], up[c, t] = (
                        x, pltpu.roll(x, 1, 1), pltpu.roll(x, LANES - 1, 1))

            for c in range(width):
                wn, wso = gn[c, flat(i), :], gs[c, flat(i), :]
                ww, we = gw[c, flat(i), :], ge[c, flat(i), :]
                out = []
                for t in range(steps):
                    for b in (c - 1) % width, c, (c + 1) % width:
                        fetch(b, t)
                    left = jnp.where(first, down[(c - 1) % width, t], down[c, t])
                    right = jnp.where(last, up[(c + 1) % width, t], up[c, t])
                    out.append(
                        wn * src[t, c, near(i, -1), :] + wso * src[t, c, near(i, 1), :]
                        + (ww * left + we * right))
                term = use(c, i, [xs[c, t] for t in range(steps)], out)
                if term is not None and c < own:
                    total = total + term
            return total
        return lax.fori_loop(0, blocks // 2, lambda i, v: block(2 * i + 1, block(2 * i, v)), zero)

    def precondition(q):
        def one(c, i, x, g):
            for t in range(steps):
                abuf[t, c, at(i), :] = 0.5 * (x[t] + g[t])

        def two(c, i, x, g):
            for t in range(steps):
                bbuf[t, c, at(i), :] = 0.125 * tau[t, c, at(i), :] + g[t]

        def three(c, i, x, g):
            term = zero
            for t in range(steps):
                v = tau[t, c, at(i), :]
                y = 0.75 * v + g[t]
                q[t, c, at(i), :] = y
                term = term + v * y
            return term

        sweep(tau, one)
        sweep(abuf, two)
        return sweep(bbuf, three)

    def operate(q):
        def use(c, i, x, g):
            shrink = inv[c, flat(i), :]
            term = zero
            for t in range(steps):
                y = x[t] - g[t]
                if t:
                    y = y - shrink * x[t - 1]
                tau[steps - 1 - t, c, at(i), :] = y
                term = term + y * x[steps - 1 - t]
            return term
        return sweep(q, use)

    precondition(q0)
    m1 = operate(q0)
    m2 = precondition(q1)
    m3 = operate(q1)
    m4 = precondition(q2)
    m5 = operate(q2)

    def norm_one(c, i, x, g):
        term = zero
        for t in range(steps):
            abuf[t, c, at(i), :] = g[t]
            term = term + (x[t] * (0.75 * x[t] + 0.125 * g[t]) + 0.5 * (g[t] * g[t]))
        return term

    def norm_two(c, i, x, g):
        term = zero
        for t in range(steps):
            term = term + 0.5 * (x[t] * g[t])
        return term

    m6 = sweep(tau, norm_one) + sweep(abuf, norm_two)

    row = jnp.zeros((1, LANES), jnp.float32)
    lane1 = lax.broadcasted_iota(jnp.int32, (1, LANES), 1)
    for j, m in enumerate((m1, m2, m3, m4, m5, m6)):
        value = jnp.sum(jnp.sum(m, axis=0, keepdims=True), axis=1, keepdims=True)
        row = jnp.where(lane1 == j, value, row)
    part[...] = row
    red[me] = row
    peers(lambda dt, ds: r_copy(dt, ds).start())
    await_bytes(red.at[pl.ds(0, n - 1)], r_sem.at[1])
    total = lax.fori_loop(0, n, lambda j, acc: acc + red[j], jnp.zeros((1, LANES), jnp.float32))
    n1, n2, n3, n4, n5, n6 = [
        jnp.sum(jnp.where(lane1 == j, total, 0.0), axis=1, keepdims=True) for j in range(6)]

    tiny = 1e-7
    d1 = jnp.maximum(n2, 1e-37)
    l21, l31 = n3 / d1, n4 / d1
    d2 = jnp.maximum(n4 - l21 * n3, jnp.maximum(tiny * n4, 1e-37))
    e32 = n5 - l31 * n3
    l32 = e32 / d2
    d3 = jnp.maximum(n6 - l31 * n4 - l32 * e32, jnp.maximum(tiny * n6, 1e-37))
    y2 = n2 - l21 * n1
    y3 = n3 - l31 * n1 - l32 * y2
    a2 = y3 / d3
    a1 = y2 / d2 - l32 * a2
    a0 = n1 / d1 - l21 * a1 - l31 * a2

    def finish(i):
        for c in range(own):
            s = scl[c, at(i), :]
            s0, s1, s2 = a0 * s, a1 * s, a2 * s
            for t in range(steps):
                res[t, c, flat(i), :] = (
                    s0 * q0[t, c, at(i), :] + s1 * q1[t, c, at(i), :]
                    + s2 * q2[t, c, at(i), :])

    loop(0, blocks, finish)
    own_out = pltpu.make_async_copy(
        res_piece(mt, ms), out_hbm.at[:, pl.ds(me * own, own)], o_sem.at[1])
    own_out.start()
    peers(lambda dt, ds: o_copy(dt, ds).start())
    await_bytes(kstage.at[pl.ds(0, nsp - 1)], k_sem.at[0])
    await_bytes(fstage.at[:, pl.ds(0, n - 1)], f_sem.at[0])
    await_bytes(red.at[pl.ds(0, n - 1)], r_sem.at[0])
    await_bytes(out_hbm, o_sem.at[1])
    await_bytes(out_hbm.at[:, pl.ds(0, (n - 1) * own)], o_sem.at[0])


def solution(mesh):
    ntm, nsp = mesh.shape["tm"], mesh.shape["space"]
    n = ntm * nsp

    def body(forcing, conductivity):
        tl, rows, columns = forcing.shape
        tiles = columns // LANES
        own = tiles // n
        width = own + 1
        steps, nx = tl * ntm, rows * nsp
        f = forcing.reshape(tl, rows, n, own, LANES).transpose(0, 2, 3, 1, 4)
        k = conductivity.reshape(rows, n, own, LANES).transpose(1, 2, 0, 3)
        padded = pltpu.VMEM((width, nx + 2 * SUB, LANES), jnp.float32)
        plain = pltpu.VMEM((width, nx, LANES), jnp.float32)
        field = pltpu.VMEM((steps, width, nx + 2 * SUB, LANES), jnp.float32)
        dma = pltpu.SemaphoreType.DMA
        f, k = (pltpu.with_memory_space_constraint(x, pltpu.HBM) for x in (f, k))
        out = pl.pallas_call(
            functools.partial(kernel, ntm, nsp),
            out_shape=jax.ShapeDtypeStruct((tl, tiles, rows, LANES), jnp.float32),
            in_specs=[pl.BlockSpec(memory_space=pltpu.HBM)] * 2,
            out_specs=pl.BlockSpec(memory_space=pl.ANY),
            scratch_shapes=[
                pltpu.VMEM((tl, n, width, rows, LANES), jnp.float32),
                pltpu.VMEM((n, own, rows, LANES), jnp.float32),
                pltpu.VMEM((nsp, width, rows, LANES), jnp.float32),
                field, padded, padded, plain, plain, plain, plain, plain,
                field, field, field, field, field, field,
                pltpu.VMEM((steps, own, nx, LANES), jnp.float32),
                pltpu.VMEM((1, LANES), jnp.float32),
                pltpu.VMEM((n, 1, LANES), jnp.float32),
                dma((2,)), dma((2,)), dma((2,)), dma((2,)), dma((3,)),
            ],
            compiler_params=pltpu.CompilerParams(
                collective_id=0, has_side_effects=True, vmem_limit_bytes=24 * 1024 * 1024),
        )(f, k)
        return out.transpose(0, 2, 1, 3).reshape(tl, rows, columns)

    return jax.shard_map(
        body,
        mesh=mesh,
        in_specs=(P("tm", "space", None), P("space", None)),
        out_specs=P("tm", "space", None),
        check_vma=False,
    )
```

```python
import functools

import jax
import jax.numpy as jnp
from jax import lax
from jax.experimental import pallas as pl
from jax.experimental.pallas import tpu as pltpu
from jax.sharding import PartitionSpec as P

MESH = pl.DeviceIdType.MESH
LANES = 128
SUB = 8


def kernel(
    ntm, nsp, f_hbm, k_hbm, out_hbm,
    fstage, kloc, kstage, fwin, kwin, scl, inv, gn, gs, gw, ge, tau, abuf, bbuf, q0, q1, q2, res, part, red,
    f_sem, k_sem, r_sem, o_sem, own_sem,
):
    n = ntm * nsp
    mt, ms = lax.axis_index("tm"), lax.axis_index("space")
    me = mt * nsp + ms
    tl, _, own, rows, _ = f_hbm.shape
    steps, width = fwin.shape[0], fwin.shape[1]
    nx = scl.shape[1] - 2 * SUB
    blocks = nx // SUB

    def strip(s):
        return pl.ds(pl.multiple_of(SUB + s * rows, SUB), rows)

    def send(src, dst, sems, dt, ds):
        return pltpu.make_async_remote_copy(
            src_ref=src, dst_ref=dst, send_sem=sems.at[0], recv_sem=sems.at[1],
            device_id=(dt, ds), device_id_type=MESH)

    def f_copy(dt, ds):
        return send(fstage.at[:, dt * nsp + ds],
                    fwin.at[pl.ds(mt * tl, tl), :, strip(ms)], f_sem, dt, ds)

    def k_copy(dt, ds):
        return send(kstage.at[ds], kwin.at[:, strip(ms)], k_sem, dt, ds)

    def r_copy(dt, ds):
        return send(part, red.at[me], r_sem, dt, ds)

    def res_piece(dt, ds):
        return res.at[pl.ds(dt * tl, tl), :, pl.ds(pl.multiple_of(ds * rows, SUB), rows)]

    def o_copy(dt, ds):
        return send(res_piece(dt, ds), out_hbm.at[:, pl.ds(me * own, own)], o_sem, dt, ds)

    def await_bytes(ref, sem):
        pltpu.make_async_copy(ref, ref, sem).wait()

    def loop(low, high, act):
        def step(j, carry):
            act(j)
            return carry
        lax.fori_loop(low, high, step, 0)

    def turn(at, by, size):
        moved = at + by
        return jnp.where(moved >= size, moved - size, moved)

    def peers(act):
        for js in sorted(range(nsp), key=lambda j: abs(j - nsp // 2)):
            ds = turn(ms, js, nsp)
            for jt in range(ntm):
                if js or jt:
                    act(turn(mt, jt, ntm), ds)

    def side_peers(act):
        for js in range(1, nsp):
            act(mt, turn(ms, js, nsp))

    barrier = pltpu.get_barrier_semaphore()
    peers(lambda dt, ds: pl.semaphore_signal(
        barrier, inc=1, device_id=(dt, ds), device_id_type=MESH))
    loads = [
        pltpu.make_async_copy(f_hbm, fstage.at[:, :, pl.ds(0, own)], own_sem.at[0]),
        pltpu.make_async_copy(k_hbm, kloc, own_sem.at[1]),
        pltpu.make_async_copy(
            k_hbm.at[pl.ds(mt * nsp, nsp)], kstage.at[:, pl.ds(0, own)], own_sem.at[2]),
    ]
    for load in loads:
        load.start()
    zero = jnp.zeros((SUB, LANES), jnp.float32)
    for edge in (0, SUB + nx):
        for c in range(width):
            for ref in (kwin, scl):
                ref[c, edge:edge + SUB, :] = zero
            for ref in (tau, abuf, bbuf, q0, q1, q2):
                for s in range(steps):
                    ref[s, c, edge:edge + SUB, :] = zero
    lane = lax.broadcasted_iota(jnp.int32, (SUB, LANES), 1)
    first, last, ahead = lane == 0, lane == LANES - 1, lane < LANES // 2

    def beside(d, right, left):
        return jnp.where(ahead, right * jnp.where(d < n - 1, 1.0, 0.0),
                         left * jnp.where(d > 0, 1.0, 0.0))

    def after(d):
        return jnp.minimum(d + 1, n - 1)

    def before(d):
        return jnp.maximum(d - 1, 0)

    for load in loads:
        load.wait()

    def overlap_k(s):
        d = mt * nsp + s
        for r in range(0, rows, SUB):
            kstage[s, own, r:r + SUB, :] = beside(
                d, kloc[after(d), 0, r:r + SUB, :], kloc[before(d), own - 1, r:r + SUB, :])

    def overlap_f(d):
        for t in range(tl):
            for r in range(0, rows, SUB):
                fstage[t, d, own, r:r + SUB, :] = beside(
                    d, fstage[t, after(d), 0, r:r + SUB, :],
                    fstage[t, before(d), own - 1, r:r + SUB, :])

    loop(0, nsp, overlap_k)
    loop(0, n, overlap_f)
    own_k = pltpu.make_async_copy(kstage.at[ms], kwin.at[:, strip(ms)], k_sem.at[1])
    own_f = pltpu.make_async_copy(
        fstage.at[:, me], fwin.at[pl.ds(mt * tl, tl), :, strip(ms)], f_sem.at[1])
    pl.semaphore_wait(barrier, n - 1)

    side_peers(lambda dt, ds: k_copy(dt, ds).start())
    peers(lambda dt, ds: f_copy(dt, ds).start())
    own_k.start()
    own_f.start()
    await_bytes(kwin.at[:, pl.ds(SUB, nx)], k_sem.at[1])

    def lefts(xs):
        turned = [pltpu.roll(x, 1, 1) for x in xs]
        return [jnp.where(first, turned[c - 1], turned[c]) for c in range(width)]

    def rights(xs):
        turned = [pltpu.roll(x, LANES - 1, 1) for x in xs]
        return [jnp.where(last, turned[(c + 1) % width], turned[c]) for c in range(width)]

    def near(i, offset):
        return pl.ds(SUB + SUB * i + offset, SUB)

    def at(i):
        return pl.ds(pl.multiple_of(SUB + SUB * i, SUB), SUB)

    def flat(i):
        return pl.ds(pl.multiple_of(SUB * i, SUB), SUB)

    inside = beside(me, jnp.ones((SUB, LANES), jnp.float32), jnp.ones((SUB, LANES), jnp.float32))

    def weights_first(i):
        ks = [kwin[c, at(i), :] for c in range(width)]
        for c, (k, l, r) in enumerate(zip(ks, lefts(ks), rights(ks))):
            up, down = kwin[c, near(i, -1), :], kwin[c, near(i, 1), :]
            diag = 1.0 + 0.5 * (k + up) + 0.5 * (k + down) + 0.5 * (k + l) + 0.5 * (k + r)
            scale = 1.0 / jnp.sqrt(diag)
            scl[c, at(i), :] = scale * inside if c == own else scale
            inv[c, flat(i), :] = 1.0 / diag

    def weights_second(i):
        ks = [kwin[c, at(i), :] for c in range(width)]
        ss = [scl[c, at(i), :] for c in range(width)]
        quads = zip(ks, lefts(ks), rights(ks), ss, lefts(ss), rights(ss))
        for c, (k, kl, kr, s, sl, sr) in enumerate(quads):
            half = 0.5 * s
            gn[c, flat(i), :] = half * (k + kwin[c, near(i, -1), :]) * scl[c, near(i, -1), :]
            gs[c, flat(i), :] = half * (k + kwin[c, near(i, 1), :]) * scl[c, near(i, 1), :]
            gw[c, flat(i), :] = half * (k + kl) * sl
            ge[c, flat(i), :] = half * (k + kr) * sr

    loop(0, blocks, weights_first)
    loop(0, blocks, weights_second)

    await_bytes(fwin.at[:, :, pl.ds(SUB, nx)], f_sem.at[1])

    def scale_in(i):
        for c in range(width):
            s = scl[c, at(i), :]
            for t in range(steps):
                tau[t, c, at(i), :] = s * fwin[steps - 1 - t, c, at(i), :]

    loop(0, blocks, scale_in)

    def sweep(src, use):
        def block(i, total):
            xs, down, up = {}, {}, {}

            def fetch(c, t):
                if (c, t) not in xs:
                    x = src[t, c, at(i), :]
                    xs[c, t], down[c, t], up[c, t] = (
                        x, pltpu.roll(x, 1, 1), pltpu.roll(x, LANES - 1, 1))

            for c in range(width):
                wn, wso = gn[c, flat(i), :], gs[c, flat(i), :]
                ww, we = gw[c, flat(i), :], ge[c, flat(i), :]
                out = []
                for t in range(steps):
                    for b in (c - 1) % width, c, (c + 1) % width:
                        fetch(b, t)
                    left = jnp.where(first, down[(c - 1) % width, t], down[c, t])
                    right = jnp.where(last, up[(c + 1) % width, t], up[c, t])
                    out.append(
                        wn * src[t, c, near(i, -1), :] + wso * src[t, c, near(i, 1), :]
                        + (ww * left + we * right))
                term = use(c, i, [xs[c, t] for t in range(steps)], out)
                if term is not None and c < own:
                    total = total + term
            return total
        group = 8 if blocks % 8 == 0 else 1

        def several(i, total):
            for j in range(group):
                total = block(group * i + j, total)
            return total

        return lax.fori_loop(0, blocks // group, several, zero)

    def precondition(q):
        def one(c, i, x, g):
            for t in range(steps):
                abuf[t, c, at(i), :] = 0.5 * (x[t] + g[t])

        def two(c, i, x, g):
            for t in range(steps):
                bbuf[t, c, at(i), :] = 0.125 * tau[t, c, at(i), :] + g[t]

        def three(c, i, x, g):
            term = zero
            for t in range(steps):
                v = tau[t, c, at(i), :]
                y = 0.75 * v + g[t]
                q[t, c, at(i), :] = y
                term = term + v * y
            return term

        sweep(tau, one)
        sweep(abuf, two)
        return sweep(bbuf, three)

    def operate(q):
        def use(c, i, x, g):
            shrink = inv[c, flat(i), :]
            term = zero
            for t in range(steps):
                y = x[t] - g[t]
                if t:
                    y = y - shrink * x[t - 1]
                tau[steps - 1 - t, c, at(i), :] = y
                term = term + y * x[steps - 1 - t]
            return term
        return sweep(q, use)

    precondition(q0)
    m1 = operate(q0)
    m2 = precondition(q1)
    m3 = operate(q1)
    m4 = precondition(q2)
    m5 = operate(q2)

    def norm_one(c, i, x, g):
        term = zero
        for t in range(steps):
            abuf[t, c, at(i), :] = g[t]
            term = term + (x[t] * (0.75 * x[t] + 0.125 * g[t]) + 0.5 * (g[t] * g[t]))
        return term

    def norm_two(c, i, x, g):
        term = zero
        for t in range(steps):
            term = term + 0.5 * (x[t] * g[t])
        return term

    m6 = sweep(tau, norm_one) + sweep(abuf, norm_two)

    row = jnp.zeros((1, LANES), jnp.float32)
    lane1 = lax.broadcasted_iota(jnp.int32, (1, LANES), 1)
    for j, m in enumerate((m1, m2, m3, m4, m5, m6)):
        value = jnp.sum(jnp.sum(m, axis=0, keepdims=True), axis=1, keepdims=True)
        row = jnp.where(lane1 == j, value, row)
    part[...] = row
    red[me] = row
    peers(lambda dt, ds: r_copy(dt, ds).start())
    await_bytes(red.at[pl.ds(0, n - 1)], r_sem.at[1])
    total = lax.fori_loop(0, n, lambda j, acc: acc + red[j], jnp.zeros((1, LANES), jnp.float32))
    n1, n2, n3, n4, n5, n6 = [
        jnp.sum(jnp.where(lane1 == j, total, 0.0), axis=1, keepdims=True) for j in range(6)]

    tiny = 1e-7
    d1 = jnp.maximum(n2, 1e-37)
    l21, l31 = n3 / d1, n4 / d1
    d2 = jnp.maximum(n4 - l21 * n3, jnp.maximum(tiny * n4, 1e-37))
    e32 = n5 - l31 * n3
    l32 = e32 / d2
    d3 = jnp.maximum(n6 - l31 * n4 - l32 * e32, jnp.maximum(tiny * n6, 1e-37))
    y2 = n2 - l21 * n1
    y3 = n3 - l31 * n1 - l32 * y2
    a2 = y3 / d3
    a1 = y2 / d2 - l32 * a2
    a0 = n1 / d1 - l21 * a1 - l31 * a2

    def finish(i):
        for c in range(own):
            s = scl[c, at(i), :]
            s0, s1, s2 = a0 * s, a1 * s, a2 * s
            for t in range(steps):
                res[t, c, flat(i), :] = (
                    s0 * q0[t, c, at(i), :] + s1 * q1[t, c, at(i), :]
                    + s2 * q2[t, c, at(i), :])

    loop(0, blocks, finish)
    own_out = pltpu.make_async_copy(
        res_piece(mt, ms), out_hbm.at[:, pl.ds(me * own, own)], o_sem.at[1])
    own_out.start()
    peers(lambda dt, ds: o_copy(dt, ds).start())
    await_bytes(kstage.at[pl.ds(0, nsp - 1)], k_sem.at[0])
    await_bytes(fstage.at[:, pl.ds(0, n - 1)], f_sem.at[0])
    await_bytes(red.at[pl.ds(0, n - 1)], r_sem.at[0])
    await_bytes(out_hbm, o_sem.at[1])
    await_bytes(out_hbm.at[:, pl.ds(0, (n - 1) * own)], o_sem.at[0])


def solution(mesh):
    ntm, nsp = mesh.shape["tm"], mesh.shape["space"]
    n = ntm * nsp

    def body(forcing, conductivity):
        tl, rows, columns = forcing.shape
        tiles = columns // LANES
        own = tiles // n
        width = own + 1
        steps, nx = tl * ntm, rows * nsp
        f = forcing.reshape(tl, rows, n, own, LANES).transpose(0, 2, 3, 1, 4)
        k = conductivity.reshape(rows, n, own, LANES).transpose(1, 2, 0, 3)
        padded = pltpu.VMEM((width, nx + 2 * SUB, LANES), jnp.float32)
        plain = pltpu.VMEM((width, nx, LANES), jnp.float32)
        field = pltpu.VMEM((steps, width, nx + 2 * SUB, LANES), jnp.float32)
        dma = pltpu.SemaphoreType.DMA
        f, k = (pltpu.with_memory_space_constraint(x, pltpu.HBM) for x in (f, k))
        out = pl.pallas_call(
            functools.partial(kernel, ntm, nsp),
            out_shape=jax.ShapeDtypeStruct((tl, tiles, rows, LANES), jnp.float32),
            in_specs=[pl.BlockSpec(memory_space=pltpu.HBM)] * 2,
            out_specs=pl.BlockSpec(memory_space=pl.ANY),
            scratch_shapes=[
                pltpu.VMEM((tl, n, width, rows, LANES), jnp.float32),
                pltpu.VMEM((n, own, rows, LANES), jnp.float32),
                pltpu.VMEM((nsp, width, rows, LANES), jnp.float32),
                field, padded, padded, plain, plain, plain, plain, plain,
                field, field, field, field, field, field,
                pltpu.VMEM((steps, own, nx, LANES), jnp.float32),
                pltpu.VMEM((1, LANES), jnp.float32),
                pltpu.VMEM((n, 1, LANES), jnp.float32),
                dma((2,)), dma((2,)), dma((2,)), dma((2,)), dma((3,)),
            ],
            compiler_params=pltpu.CompilerParams(
                collective_id=0, has_side_effects=True, vmem_limit_bytes=24 * 1024 * 1024),
        )(f, k)
        return out.transpose(0, 2, 1, 3).reshape(tl, rows, columns)

    return jax.shard_map(
        body,
        mesh=mesh,
        in_specs=(P("tm", "space", None), P("space", None)),
        out_specs=P("tm", "space", None),
        check_vma=False,
    )
```
